768 devices in a mesh: grp: 48 (over z, x), sub: 16 (over y, core).
Axes of the slice: x: 4, y: 8, z: 12, core: 2. Of those that a mesh axis runs over, the one named last changes fastest.
Arguments:
- load: float32 [48, 16, 15, 384], P('grp', 'sub'), may hold values from -6 to 6
- couple: bfloat16 [48, 16, 4, 15, 15, 384], P('grp', 'sub'), may hold values from -1 to 6
- face_link: int32 [48, 16, 3, 384], P('grp', 'sub'), may hold values from 0 to 383, as said below
- face_count: int32 [48, 16], P('grp', 'sub'), may hold values from 256 to 384, as said below
- slot_face: int32 [48, 16, 16, 32], P('grp', 'sub'), may hold values from 0 to 383, as said below
- pair_count: int32 [48, 16, 16], P('grp', 'sub'), may hold values from 0 to 32, as said below
- basis: float32 [48, 16, 64, 15, 384], P('grp', 'sub'), may hold values from -0.0390625 to 0.0390625
- coarse_inverse: float32 [48, 16, 64, 64], P('grp', 'sub'), may hold values from -0.25 to 1.65
- coarse_block: float32 [48, 16, 6, 64, 64], P('grp', 'sub'), may hold values from -0.15625 to 0.15625
- coarse_link: int32 [48, 16, 6], P('grp', 'sub'), may hold values from 0 to 767, as said below
Outputs:
- trace_field: float32 [48, 16, 15, 384], P('grp', 'sub')
- robin_data: float32 [48, 16, 15, 384], P('grp', 'sub')
- coarse_coef: float32 [48, 16, 64], P('grp', 'sub')
The draws below stay inside these ranges and needn't reach their ends.
Inputs may be any that keep to these rules, and one draw needn't show every extreme that they name: Subdomain (g, i) has live face blocks 0 to face_count[g, i] - 1; the rest are padding. Some subdomain has all 384 live. pair_count[g, i, j] equals pair_count[g, j, i], is 0 for j = i and otherwise 1 or more, a quarter of 32 or more, rounded down; every subdomain has exactly one peer with 32, and all its other peers have half of 32 or fewer. `slot_face`: for c < pair_count[g, i, j], slot c toward j names a live face block of i that i shares with j, the same face that slot c of j toward i names on j's side; these faces are distinct within a subdomain. Other slots name any face block. `face_link`: linked face blocks are live and differ from the face block itself. `coarse_link`: the 6 coarse neighbours of subdomain (g, i) are distinct, differ from it, and lie in groups g - 1, g or g + 1.
All inputs are finite; a program needn't handle non-finite values.
Results may differ from the reference program's by a relative error of at most 0.0015.
Values sent between devices are 32-bit elements; how exact they have to be, the bound alone decides.
No kernel may reach another device: no remote copies, remote signals or barrier semaphores. Data moves between devices by JAX's collectives and lax.ppermute only.
A program may use at most 32 MiB of HBM per device.

```python
import jax
import jax.numpy as jnp
from jax import lax

TRACE = 15
FB = 384
CAP = 32
LINKS = 3
CVEC = 64
KC = 6
ITERS = 3
SWEEPS = 2
CSWEEPS = 2
GROUPS = 48
PEERS = 16


def face_counts(key):
    count_key = jax.random.fold_in(key, 11)
    interface_most = CAP + (PEERS - 2) * (CAP // 2)
    lower = max(interface_most, FB // 2)
    counts = jax.random.randint(count_key, (GROUPS * PEERS,), lower, FB + 1)
    chosen = jax.random.randint(jax.random.fold_in(count_key, 1), (), 0, GROUPS * PEERS)
    counts = jnp.where(jnp.arange(GROUPS * PEERS) == chosen, FB, counts)
    return counts.reshape(GROUPS, PEERS).astype(jnp.int32)


def shuffle(group_key):
    return jax.random.permutation(group_key, PEERS)


def pair_counts(key):
    light_low = max(1, CAP // 4)
    light_count = jax.random.randint(jax.random.fold_in(key, 23), (GROUPS, PEERS, PEERS), light_low, CAP // 2 + 1)
    row_index = jnp.arange(PEERS)[:, None]
    col_index = jnp.arange(PEERS)[None, :]
    symmetric = jnp.where(row_index < col_index, light_count, jnp.swapaxes(light_count, 1, 2))
    group_keys = jax.random.split(jax.random.fold_in(key, 29), GROUPS)
    orders = jax.vmap(shuffle)(group_keys).astype(jnp.int32)
    position = jnp.argsort(orders, axis=1).astype(jnp.int32)
    partner = jnp.take_along_axis(orders, jnp.bitwise_xor(position, 1), axis=1)
    heavy_pair = partner[:, :, None] == col_index[None]
    result = jnp.where(heavy_pair, CAP, symmetric)
    result = jnp.where(row_index == col_index, 0, result)
    return result.astype(jnp.int32)


def draw_face_count(key, part):
    return face_counts(key)


def draw_pair_count(key, part):
    return pair_counts(key)


def draw_slot_face(key, part):
    counts = face_counts(key)
    pairs = pair_counts(key)
    face_ids = jnp.arange(FB, dtype=jnp.int32)
    scores = jax.random.randint(jax.random.fold_in(key, 37), (GROUPS, PEERS, FB), 0, 2 ** 19) * FB + face_ids
    active = face_ids[None, None, :] < counts[:, :, None]
    scores = jnp.where(active, scores, 2 ** 30 + face_ids)
    ranking = jnp.argsort(scores, axis=-1).astype(jnp.int32)
    offsets = jnp.cumsum(pairs, axis=-1) - pairs
    position = offsets[..., None] + jnp.arange(CAP, dtype=jnp.int32)
    position = jnp.minimum(position, FB - 1).reshape(GROUPS, PEERS, PEERS * CAP)
    chosen_faces = jnp.take_along_axis(ranking, position, axis=-1)
    return chosen_faces.reshape(GROUPS, PEERS, PEERS, CAP).astype(jnp.int32)


def draw_face_link(key, part):
    counts = face_counts(key)
    random_ints = jax.random.randint(jax.random.fold_in(key, 41), (GROUPS, PEERS, LINKS, FB), 0, 2 ** 20)
    face_ids = jnp.arange(FB, dtype=jnp.int32)
    live_count = counts[:, :, None, None]
    face_pick = (face_ids + 1 + random_ints % (live_count - 1)) % live_count
    return face_pick.astype(jnp.int32)


def draw_coarse_link(key, part):
    candidate = jnp.arange(3 * PEERS, dtype=jnp.int32)
    group_ids = jnp.arange(GROUPS, dtype=jnp.int32)[:, None, None]
    sub_ids = jnp.arange(PEERS, dtype=jnp.int32)[None, :, None]
    near_group = group_ids - 1 + candidate // PEERS
    near_sub = candidate % PEERS
    invalid = (near_group < 0) | (near_group >= GROUPS) | (near_group == group_ids) & (near_sub == sub_ids)
    scores = jax.random.randint(jax.random.fold_in(key, 53), (GROUPS, PEERS, 3 * PEERS), 0, 2 ** 20) * (3 * PEERS) + candidate
    scores = jnp.where(invalid, 2 ** 30 + candidate, scores)
    picked = jnp.argsort(scores, axis=-1)[..., :KC].astype(jnp.int32)
    global_ids = (group_ids - 1 + picked // PEERS) * PEERS + picked % PEERS
    return global_ids.astype(jnp.int32)


def draw_couple(key, part):
    full_shape = (GROUPS, PEERS, LINKS + 1, TRACE, TRACE, FB)
    noise_part = jnp.clip(0.2 * jax.random.normal(jax.random.fold_in(key, 61), full_shape, jnp.float32), -1.0, 1.0)
    diagonal = jax.random.uniform(jax.random.fold_in(key, 67), (GROUPS, PEERS, 1, TRACE, 1, FB), jnp.float32, 3.0, 5.0)
    identity = jnp.eye(TRACE, dtype=jnp.float32)[:, :, None]
    first_block = (jnp.arange(LINKS + 1) == 0).astype(jnp.float32)[:, None, None, None]
    return (noise_part + first_block * identity * diagonal).astype(jnp.bfloat16)


def draw_coarse_inverse(key, part):
    full_shape = (GROUPS, PEERS, CVEC, CVEC)
    noise_part = jnp.clip(0.04 * jax.random.normal(jax.random.fold_in(key, 71), full_shape, jnp.float32), -0.25, 0.25)
    diagonal = jax.random.uniform(jax.random.fold_in(key, 73), (GROUPS, PEERS, CVEC, 1), jnp.float32, 0.6, 1.4)
    identity = jnp.eye(CVEC, dtype=jnp.float32)
    return (noise_part + identity * diagonal).astype(jnp.float32)


def shard_levels(stream_key, shape, shards, low, top_value):
    gain, own = 1.0, jax.random.fold_in(stream_key, 6)
    for axis_at, parts in shards:
        draws = jnp.exp(jax.random.uniform(jax.random.fold_in(own, axis_at), (parts,), jnp.float32, low / len(shards), top_value / len(shards)))
        gain = gain * jnp.repeat(draws, shape[axis_at] // parts).reshape([-1 if axis == axis_at else 1 for axis in range(len(shape))])
    return gain


def bell_draw(own_key, dims, width, most, pieces=(), held_as=jnp.bfloat16):
    entries = width * jax.random.normal(own_key, dims, jnp.float32)
    if pieces:
        entries = entries * shard_levels(own_key, dims, pieces, -0.22, 0.18)
    return jnp.clip(entries, -most, most).astype(held_as)


def setup_inputs(seed: int = 0) -> dict:
    streams_of = jax.random.split(jax.random.key(seed), 11)
    return {
        "load": bell_draw(streams_of[0], (GROUPS, PEERS, TRACE, FB), 1.0, 6.0, ((0, 48), (1, 16)), jnp.float32),
        "couple": draw_couple(jax.random.fold_in(streams_of[10], 71), 0),
        "face_link": draw_face_link(jax.random.fold_in(streams_of[10], 71), 0),
        "face_count": draw_face_count(jax.random.fold_in(streams_of[10], 71), 0),
        "slot_face": draw_slot_face(jax.random.fold_in(streams_of[10], 71), 0),
        "pair_count": draw_pair_count(jax.random.fold_in(streams_of[10], 71), 0),
        "basis": bell_draw(streams_of[6], (GROUPS, PEERS, CVEC, TRACE, FB), (4 * TRACE * FB) ** -0.5, 0.0390625, ((0, 48), (1, 16)), jnp.float32),
        "coarse_inverse": draw_coarse_inverse(jax.random.fold_in(streams_of[10], 71), 0),
        "coarse_block": bell_draw(streams_of[8], (GROUPS, PEERS, KC, CVEC, CVEC), (4 * KC * CVEC) ** -0.5, 0.15625, ((0, 48), (1, 16)), jnp.float32),
        "coarse_link": draw_coarse_link(jax.random.fold_in(streams_of[10], 71), 0),
    }


robin_weight = 1.0
omega_step = 0.2
highest = lax.Precision.HIGHEST


def couple_apply(couple, face_links, trace_rows, live_mask, interface):
    linked = jnp.moveaxis(trace_rows[:, face_links], 1, 0)
    stacked = jnp.concatenate([trace_rows[None], linked], axis=0)
    product = jnp.sum(couple * stacked[:, None, :, :], axis=(0, 2))
    return live_mask * (product + robin_weight * interface * trace_rows)


def masks_for(own_count, own_slots, own_pairs):
    live_mask = (jnp.arange(FB) < own_count).astype(jnp.float32)
    valid_slots = jnp.arange(CAP)[None, :] < own_pairs[:, None]
    counted = jnp.zeros((FB,), jnp.float32).at[own_slots].add(valid_slots.astype(jnp.float32))
    return live_mask, jnp.minimum(counted, 1.0), valid_slots


def local_phase(load_rows, couple, face_links, live_mask, interface, basis_rows, trace_field, robin_data):
    for sweep_index in range(SWEEPS):
        residual = live_mask * (load_rows + robin_data) - couple_apply(couple, face_links, trace_field, live_mask, interface)
        trace_field = trace_field + omega_step * residual
    residual = live_mask * (load_rows + robin_data) - couple_apply(couple, face_links, trace_field, live_mask, interface)
    restricted = jnp.dot(basis_rows.reshape(basis_rows.shape[0], -1), residual.reshape(-1), precision=highest)
    return trace_field, restricted


def run_groups(operands):
    return jax.vmap(local_phase)(*operands)


def take_slots(trace_rows, slot_rows):
    return trace_rows[:, slot_rows]


def add_slots(arrivals, slot_rows):
    return jnp.zeros((TRACE, FB), jnp.float32).at[:, slot_rows].add(arrivals)


def reference(load, couple, face_link, face_count, slot_face, pair_count, basis, coarse_inverse, coarse_block, coarse_link):
    live_mask, interface, valid_slots = jax.vmap(jax.vmap(masks_for))(face_count, slot_face, pair_count)
    trace_field = jnp.zeros(load.shape, jnp.float32)
    robin_data = jnp.zeros(load.shape, jnp.float32)
    coefficients = jnp.zeros((GROUPS, PEERS, CVEC), jnp.float32)
    for outer_step in range(ITERS):
        trace_field, restricted = lax.map(run_groups, (load, couple, face_link, live_mask, interface, basis, trace_field, robin_data))
        coarse_start = jnp.einsum("gpvw,gpw->gpv", coarse_inverse, restricted, precision=highest)
        coefficients = coarse_start
        for inner_step in range(CSWEEPS):
            flattened = coefficients.reshape(-1, CVEC)
            gathered = flattened[coarse_link]
            coupled = jnp.einsum("gpkvw,gpkw->gpv", coarse_block, gathered, precision=highest)
            coefficients = coarse_start - jnp.einsum("gpvw,gpw->gpv", coarse_inverse, coupled, precision=highest)
        correction = jnp.einsum("gpv,gpvaf->gpaf", coefficients, basis, precision=highest)
        trace_field = trace_field + live_mask[:, :, None, :] * correction
        outgoing = 2.0 * robin_weight * trace_field - robin_data
        sent = jax.vmap(jax.vmap(take_slots))(outgoing, slot_face)
        received = jnp.transpose(sent, (0, 3, 2, 1, 4))
        received = jnp.where(valid_slots[:, :, None, :, :], received, 0.0)
        robin_data = jax.vmap(jax.vmap(add_slots))(received, slot_face)
    return trace_field, robin_data, coefficients
```

```python
import functools

import jax
import jax.numpy as jnp
from jax import lax
from jax.experimental import pallas as pl
from jax.experimental.pallas import tpu as pltpu
from jax.sharding import PartitionSpec as P

TRACE = 15
ROWS = 16
FB = 384
CAP = 32
LANES = 128
LINKS = 3
CVEC = 64
KC = 6
ITERS = 3
SWEEPS = 2

robin_weight = 1.0
omega_step = 0.2
f32 = jnp.float32


def pick(pieces, index):
    low = jnp.bitwise_and(index, LANES - 1)
    high = jnp.right_shift(index, 7)
    out = None
    for at, piece in enumerate(pieces):
        taken = jnp.take_along_axis(piece, low, axis=1, mode="promise_in_bounds")
        out = taken if out is None else jnp.where(high == at, taken, out)
    return out


def tiles_of(rows):
    return [rows[:, t * LANES : (t + 1) * LANES] for t in range(rows.shape[1] // LANES)]


def pick_faces(rows, index_row):
    pieces = tiles_of(rows)
    picked = [
        pick(pieces, jnp.broadcast_to(part, (rows.shape[0], LANES))) for part in tiles_of(index_row)
    ]
    return jnp.concatenate(picked, axis=1)


def live_row(count):
    return (lax.broadcasted_iota(jnp.int32, (1, FB), 1) < count).astype(f32)


def eye(offset):
    row = lax.broadcasted_iota(jnp.int32, (CVEC, LANES), 0)
    lane = lax.broadcasted_iota(jnp.int32, (CVEC, LANES), 1)
    return lane == row + offset


def matvec(matrix, row):
    return jnp.sum(matrix * row, axis=1, keepdims=True)


def as_row(low, high):
    spread = jnp.where(eye(0), low, 0.0) + jnp.where(eye(CVEC), high, 0.0)
    return jnp.sum(spread, axis=0, keepdims=True)


def couple_apply(couple_ref, link_ref, trace, live, interface, sum_ref):
    stacked = [trace] + [pick_faces(trace, link_ref[k : k + 1, :]) for k in range(LINKS)]
    stacked = [rows[:TRACE] for rows in stacked]
    for a in range(TRACE):
        product = stacked[0] * couple_ref[0, a].astype(f32)
        for k in range(1, LINKS + 1):
            product = product + stacked[k] * couple_ref[k, a].astype(f32)
        sum_ref[a : a + 1, :] = jnp.sum(product, axis=0, keepdims=True)
    return live * (sum_ref[...] + robin_weight * interface * trace)


def unpack_slots(arrived_ref, inverse_row):
    lane = lax.broadcasted_iota(jnp.int32, (8, LANES), 1) // CAP
    per_tile = LANES // CAP
    count = arrived_ref.shape[0] // 8 // per_tile
    halves = []
    for half in range(2):
        pieces = []
        for tile in range(count):
            joined = None
            for m in range(per_tile):
                at = (tile * per_tile + m) * 8
                block = arrived_ref[at : at + 8, :]
                place = (m + 2 * half) % per_tile
                joined = block if joined is None else jnp.where(lane == place, block, joined)
            pieces.append(joined)
        index = jnp.maximum(inverse_row, 0)
        if half:
            index = jnp.bitwise_or(
                jnp.bitwise_and(index, -LANES), jnp.bitwise_and(index + LANES // 2, LANES - 1)
            )
        picked = [
            pick(pieces, jnp.broadcast_to(part, (8, LANES))) for part in tiles_of(index)
        ]
        halves.append(jnp.concatenate(picked, axis=1))
    rows = jnp.concatenate(halves, axis=0)
    return jnp.where(inverse_row >= 0, rows, 0.0)


def restrict(basis_ref, residual, part_ref):
    residual = residual[:TRACE]
    for v in range(CVEC):
        product = basis_ref[v] * residual
        folded = product[:, :LANES] + product[:, LANES : 2 * LANES] + product[:, 2 * LANES :]
        part_ref[v : v + 1, :] = jnp.sum(folded, axis=0, keepdims=True)
    return jnp.sum(part_ref[...], axis=1, keepdims=True)


def start_coarse(blocks_ref, basis_ref, residual, part_ref, send_ref):
    column = restrict(basis_ref, residual, part_ref)
    start = matvec(blocks_ref[:CVEC, :], as_row(column, column)[:, :CVEC])
    send_ref[...] = jnp.broadcast_to(as_row(start, start), send_ref.shape)


def first_kernel(
    count_ref, pairs_ref, slots_ref, load_ref, link_ref, blocks_ref, couple_hbm, basis_hbm,
    trace_ref, inverse_ref, send_ref,
    couple_ref, basis_ref, sum_ref, part_ref, sems,
):
    couple_copy = pltpu.make_async_copy(couple_hbm, couple_ref, sems.at[0])
    basis_copy = pltpu.make_async_copy(basis_hbm, basis_ref, sems.at[1])
    couple_copy.start()
    basis_copy.start()
    live = live_row(count_ref[0, 0])
    slot = lax.broadcasted_iota(jnp.int32, (CAP, FB), 0)
    face = lax.broadcasted_iota(jnp.int32, (CAP, FB), 1)
    found = jnp.zeros((CAP, FB), jnp.int32)
    for j in range(slots_ref.shape[1]):
        named = (slots_ref[:, j : j + 1] == face) & (slot < pairs_ref[0, j])
        found = found + jnp.where(named, slot + (j * CAP + 1), 0)
    inverse = jnp.sum(found, axis=0, keepdims=True) - 1
    inverse_ref[...] = inverse
    interface = (inverse >= 0).astype(f32)
    sum_ref[...] = jnp.zeros_like(sum_ref)
    trace_ref[...] = jnp.zeros_like(trace_ref)
    source = live * load_ref[...]
    trace_ref[:TRACE, :] = source
    source = trace_ref[...]
    trace = omega_step * source
    couple_copy.wait()
    for sweep in range(1, SWEEPS):
        trace = trace + omega_step * (
            source - couple_apply(couple_ref, link_ref, trace, live, interface, sum_ref)
        )
    trace_ref[...] = trace
    residual = source - couple_apply(couple_ref, link_ref, trace, live, interface, sum_ref)
    basis_copy.wait()
    start_coarse(blocks_ref, basis_ref, residual, part_ref, send_ref)


def local_kernel(
    count_ref, arrived_ref, inverse_ref, load_ref, link_ref, blocks_ref, old_ref, couple_hbm, basis_hbm,
    trace_ref, robin_ref, send_ref,
    couple_ref, basis_ref, sum_ref, part_ref, sems,
):
    couple_copy = pltpu.make_async_copy(couple_hbm, couple_ref, sems.at[0])
    basis_copy = pltpu.make_async_copy(basis_hbm, basis_ref, sems.at[1])
    couple_copy.start()
    basis_copy.start()
    live = live_row(count_ref[0, 0])
    inverse = inverse_ref[...]
    interface = (inverse >= 0).astype(f32)
    sum_ref[...] = jnp.zeros_like(sum_ref)
    robin = unpack_slots(arrived_ref, inverse)
    robin_ref[...] = robin
    trace_ref[...] = jnp.zeros_like(trace_ref)
    trace_ref[:TRACE, :] = load_ref[...]
    source = live * (trace_ref[...] + robin)
    trace = old_ref[...]
    couple_copy.wait()
    for sweep in range(SWEEPS):
        trace = trace + omega_step * (
            source - couple_apply(couple_ref, link_ref, trace, live, interface, sum_ref)
        )
    trace_ref[...] = trace
    residual = source - couple_apply(couple_ref, link_ref, trace, live, interface, sum_ref)
    basis_copy.wait()
    start_coarse(blocks_ref, basis_ref, residual, part_ref, send_ref)


def jacobi(blocks_ref, start_row, neighbour_rows):
    total = None
    for k in range(KC):
        term = blocks_ref[pl.ds((k + 1) * CVEC, CVEC), :] * neighbour_rows[k]
        total = term if total is None else total + term
    coupled = jnp.sum(total, axis=1, keepdims=True)
    step = matvec(blocks_ref[:CVEC, :], as_row(coupled, coupled)[:, :CVEC])
    start = jnp.sum(jnp.where(eye(0)[:, :CVEC], start_row, 0.0), axis=1, keepdims=True)
    return start - step


def sweep_kernel(place_ref, own_ref, partner_ref, blocks_ref, twin_ref, send_ref, stack_ref):
    rows = own_ref.shape[0]
    stack_ref[:rows, :] = own_ref[...]
    stack_ref[rows:, :] = partner_ref[...]

    def row(which, k):
        return stack_ref[pl.ds(place_ref[which, k], 1), :][:, :CVEC]

    columns = [
        jacobi(matrices, row(which, KC), [row(which, k) for k in range(KC)])
        for which, matrices in ((0, blocks_ref), (1, twin_ref))
    ]
    send_ref[...] = jnp.broadcast_to(as_row(*columns), send_ref.shape)


def correct_kernel(
    first, last, place_ref, meta_ref, start_ref, swept_ref, blocks_ref, slots_ref, trace_ref, *rest
):
    if first:
        basis_hbm, *rest = rest
    else:
        robin_ref, basis_hbm, *rest = rest
    if last:
        out_ref, coef_ref, packed_ref, basis_ref, spread_ref, sems = rest
    else:
        out_ref, packed_ref, basis_ref, spread_ref, sems = rest
    basis_copy = pltpu.make_async_copy(basis_hbm, basis_ref, sems.at[0])
    basis_copy.start()

    def row(k):
        whole = swept_ref[pl.ds(place_ref[2, k], 1), :]
        moved = pltpu.roll(whole, CVEC, 1)
        return jnp.where(place_ref[3, k] > 0, moved, whole)[:, :CVEC]

    column = jacobi(blocks_ref, start_ref[:1, :CVEC], [row(k) for k in range(KC)])
    if last:
        coef_ref[...] = as_row(column, column)[:, :CVEC]
    spread_ref[...] = jnp.broadcast_to(column, spread_ref.shape)
    live = live_row(meta_ref[0, 0])
    basis_copy.wait()
    parts = [None] * 4
    for v in range(CVEC):
        scale = spread_ref[v : v + 1, :]
        term = basis_ref[v] * jnp.concatenate([scale] * (FB // LANES), axis=1)
        parts[v % 4] = term if parts[v % 4] is None else parts[v % 4] + term
    correction = live * ((parts[0] + parts[1]) + (parts[2] + parts[3]))
    grown = trace_ref[...]
    trace = grown[:TRACE] + correction
    if last:
        out_ref[...] = trace
    if first:
        outgoing = 2.0 * robin_weight * trace
    else:
        outgoing = 2.0 * robin_weight * trace - robin_ref[:TRACE, :]
    packed_ref[0:ROWS, :] = jnp.zeros((ROWS, LANES), f32)
    rows_ref = out_ref if not last else None
    if not last:
        rows_ref[...] = grown
        rows_ref[:TRACE, :] = trace
    pad = jnp.concatenate([outgoing, jnp.zeros((ROWS - TRACE, FB), f32)], axis=0)
    upper = tiles_of(pad[:8])
    lower = tiles_of(pad[8:])
    lane = lax.broadcasted_iota(jnp.int32, (8, LANES), 1) // CAP
    mine = lane == meta_ref[0, 1]
    for j in range(slots_ref.shape[0]):
        index = jnp.broadcast_to(slots_ref[j : j + 1, :], (8, LANES))
        packed_ref[j * 8 : (j + 1) * 8, :] = jnp.where(mine, pick(upper, index), pick(lower, index))


def robin_kernel(arrived_ref, inverse_ref, out_ref):
    out_ref[...] = unpack_slots(arrived_ref, inverse_ref[...])[:TRACE]


SMEM = pl.BlockSpec(memory_space=pltpu.SMEM)
VMEM = pl.BlockSpec(memory_space=pltpu.VMEM)
HBM = pl.BlockSpec(memory_space=pl.ANY)


def call(kernel, name, in_specs, outs, scratch, limit_mib):
    return pl.pallas_call(
        kernel,
        name=name,
        out_shape=[jax.ShapeDtypeStruct(shape, dtype) for shape, dtype in outs],
        in_specs=in_specs,
        out_specs=[VMEM] * len(outs),
        scratch_shapes=scratch,
        compiler_params=pltpu.CompilerParams(vmem_limit_bytes=limit_mib << 20),
    )


COUPLE = pltpu.VMEM((LINKS + 1, TRACE, TRACE, FB), jnp.bfloat16)
BASIS = pltpu.VMEM((CVEC, TRACE, FB), f32)


def pair_groups(groups, peers):
    return [[(2 * m + h) * peers + s for h in range(2) for s in range(peers)] for m in range(groups // 2)]


def partner_pairs(groups):
    pairs = []
    for m in range(groups // 2):
        odd, even = 2 * m + 1, (2 * m + 2) % groups
        pairs += [(odd, even), (even, odd)]
    return pairs


def body(
    load, couple, face_link, face_count, slot_face, pair_count, basis, coarse_inverse, coarse_block, coarse_link
):
    groups, peers = lax.axis_size("grp"), lax.axis_size("sub")
    group, own = lax.axis_index("grp"), lax.axis_index("sub")
    blocks = pair_groups(groups, peers)
    partners = partner_pairs(groups)
    rows = 2 * peers

    def exchange(send):
        arrived = lax.all_to_all(
            send.reshape(rows, 1, LANES), ("grp", "sub"), 0, 0, axis_index_groups=blocks, tiled=True
        )
        return arrived.reshape(rows, LANES)

    links = coarse_link[0, 0]
    tail = jnp.zeros((8, CVEC), f32).at[0, :KC].set(links.astype(f32))
    packed = jnp.concatenate(
        [coarse_inverse[0, 0], coarse_block[0, 0].reshape(KC * CVEC, CVEC), tail], axis=0
    )
    twin = lax.ppermute(packed, "grp", partners)
    twin_links = twin[(KC + 1) * CVEC, :KC].astype(jnp.int32)

    base = group // 2 * 2
    odd = group - base
    partner = jnp.where(odd == 1, (group + 1) % groups, (group + groups - 1) % groups)
    partner_base = partner // 2 * 2
    ids = jnp.stack(
        [
            jnp.concatenate([links, (group * peers + own)[None]]),
            jnp.concatenate([twin_links, (partner * peers + own)[None]]),
        ]
    )
    in_pair = ids // peers // 2 * 2 == base
    first_places = jnp.where(in_pair, ids - base * peers, rows + ids - partner_base * peers)
    first_places = jnp.clip(first_places, 0, 2 * rows - 1)
    ahead = ids[0] // peers - base
    across = (ahead < 0) | (ahead > 1)
    second_places = jnp.where(ahead > 0, peers, 0) + ids[0] % peers
    places = jnp.concatenate([first_places, second_places[None], across.astype(jnp.int32)[None]], axis=0)

    count = face_count.astype(jnp.int32)
    meta = jnp.stack([face_count[0, 0], own % (LANES // CAP)])[None]
    own_slots = slot_face[0, 0]
    wide_slots = jnp.tile(own_slots, (1, LANES // CAP))
    face_links = face_link[0, 0]
    load_rows, couple_rows, basis_rows = load[0, 0], couple[0, 0], basis[0, 0]

    field = ((ROWS, FB), f32)
    sends = ((rows, LANES), f32)
    work = [
        COUPLE,
        BASIS,
        pltpu.VMEM((ROWS, FB), f32),
        pltpu.VMEM((CVEC, LANES), f32),
        pltpu.SemaphoreType.DMA((2,)),
    ]
    arrived = robin = inverse = trace = None
    for outer_step in range(ITERS):
        first, last = outer_step == 0, outer_step == ITERS - 1
        if first:
            trace, inverse, start = call(
                first_kernel,
                "first",
                [SMEM, SMEM, VMEM, VMEM, VMEM, VMEM, HBM, HBM],
                [field, ((1, FB), jnp.int32), sends],
                work,
                16,
            )(
                count, pair_count[0], own_slots.T, load_rows, face_links, packed, couple_rows, basis_rows
            )
        else:
            trace, robin, start = call(
                local_kernel,
                "local",
                [SMEM, VMEM, VMEM, VMEM, VMEM, VMEM, VMEM, HBM, HBM],
                [field, field, sends],
                work,
                16,
            )(
                count, arrived, inverse, load_rows, face_links, packed, trace, couple_rows, basis_rows
            )
        window = exchange(start)
        beyond = lax.ppermute(window, "grp", partners)
        (swept,) = call(
            sweep_kernel,
            "sweep",
            [SMEM, VMEM, VMEM, VMEM, VMEM],
            [sends],
            [pltpu.VMEM((2 * rows, LANES), f32)],
            8,
        )(places, window, beyond, packed, twin)
        swept = exchange(swept)
        outs = [((TRACE, FB), f32), ((1, CVEC), f32)] if last else [field]
        outs = outs + [((peers * 8, LANES), f32)]
        operands = [places, meta, start, swept, packed, wide_slots, trace]
        operands += ([] if first else [robin]) + [basis_rows]
        results = call(
            functools.partial(correct_kernel, first, last),
            "correct",
            [SMEM, SMEM] + [VMEM] * (len(operands) - 3) + [HBM],
            outs,
            [BASIS, pltpu.VMEM((CVEC, LANES), f32), pltpu.SemaphoreType.DMA((1,))],
            16,
        )(*operands)
        trace, outgoing = results[0], results[-1]
        if last:
            coefficients = results[1]
        arrived = lax.all_to_all(outgoing.reshape(peers, 8, LANES), "sub", 0, 0, tiled=True)
        arrived = arrived.reshape(peers * 8, LANES)
    (robin,) = call(robin_kernel, "robin", [VMEM, VMEM], [((TRACE, FB), f32)], [], 8)(arrived, inverse)
    return (trace[None, None], robin[None, None], coefficients[None])


def solution(mesh):
    in_specs = (
        P("grp", "sub", None, None),
        P("grp", "sub", None, None, None, None),
        P("grp", "sub", None, None),
        P("grp", "sub"),
        P("grp", "sub", None, None),
        P("grp", "sub", None),
        P("grp", "sub", None, None, None),
        P("grp", "sub", None, None),
        P("grp", "sub", None, None, None),
        P("grp", "sub", None),
    )
    out_specs = (P("grp", "sub", None, None), P("grp", "sub", None, None), P("grp", "sub", None))
    return jax.shard_map(body, mesh=mesh, in_specs=in_specs, out_specs=out_specs, check_vma=False)
```

```python
import functools

import jax
import jax.numpy as jnp
from jax import lax
from jax.experimental import pallas as pl
from jax.experimental.pallas import tpu as pltpu
from jax.sharding import PartitionSpec as P

TRACE = 15
ROWS = 16
FB = 384
CAP = 32
LANES = 128
LINKS = 3
CVEC = 64
KC = 6
ITERS = 3
SWEEPS = 2

robin_weight = 1.0
omega_step = 0.2
f32 = jnp.float32


def pick(pieces, index):
    low = jnp.bitwise_and(index, LANES - 1)
    high = jnp.right_shift(index, 7)
    out = None
    for at, piece in enumerate(pieces):
        taken = jnp.take_along_axis(piece, low, axis=1, mode="promise_in_bounds")
        out = taken if out is None else jnp.where(high == at, taken, out)
    return out


def tiles_of(rows):
    return [rows[:, t * LANES : (t + 1) * LANES] for t in range(rows.shape[1] // LANES)]


def pick_faces(rows, index_row):
    pieces = tiles_of(rows)
    picked = [
        pick(pieces, jnp.broadcast_to(part, (rows.shape[0], LANES))) for part in tiles_of(index_row)
    ]
    return jnp.concatenate(picked, axis=1)


def pick_rows(blocks, index):
    low = jnp.bitwise_and(index, 7)
    high = jnp.right_shift(index, 3)
    out = None
    for at, block in enumerate(blocks):
        taken = jnp.take_along_axis(block, low, axis=0, mode="promise_in_bounds")
        out = taken if out is None else jnp.where(high == at, taken, out)
    return out


def blocks_of(ref, rows):
    return [ref[at : at + 8, :] for at in range(0, rows, 8)]


def eye(offset):
    row = lax.broadcasted_iota(jnp.int32, (CVEC, LANES), 0)
    lane = lax.broadcasted_iota(jnp.int32, (CVEC, LANES), 1)
    return lane == row + offset


def as_row(low, high=None):
    spread = jnp.where(eye(0), low, 0.0)
    if high is not None:
        spread = spread + jnp.where(eye(CVEC), high, 0.0)
    return jnp.sum(spread, axis=0, keepdims=True)


def low_lanes():
    return lax.broadcasted_iota(jnp.int32, (1, LANES), 1) < CVEC


def couple_apply(couple_ref, link_ref, trace, live, interface, stack_ref):
    stack_ref[0] = trace
    for k in range(LINKS):
        stack_ref[k + 1] = pick_faces(trace, link_ref[k])
    sums = []
    for k in range(LINKS + 1):
        total = None
        for b in range(TRACE):
            term = couple_ref[k, b].astype(f32) * stack_ref[k, b : b + 1, :]
            total = term if total is None else total + term
        sums.append(total)
    total = (sums[0] + sums[1]) + (sums[2] + sums[3])
    return live * (total + robin_weight * interface * trace[:TRACE])


def unpack_slots(arrived_ref, inverse_row):
    lane = lax.broadcasted_iota(jnp.int32, (8, LANES), 1) // CAP
    per_tile = LANES // CAP
    count = arrived_ref.shape[0] // 8 // per_tile
    halves = []
    for half in range(2):
        pieces = []
        for tile in range(count):
            joined = None
            for m in range(per_tile):
                at = (tile * per_tile + m) * 8
                block = arrived_ref[at : at + 8, :]
                place = (m + 2 * half) % per_tile
                joined = block if joined is None else jnp.where(lane == place, block, joined)
            pieces.append(joined)
        index = jnp.maximum(inverse_row, 0)
        if half:
            index = jnp.bitwise_or(
                jnp.bitwise_and(index, -LANES), jnp.bitwise_and(index + LANES // 2, LANES - 1)
            )
        picked = [
            pick(pieces, jnp.broadcast_to(part, (8, LANES))) for part in tiles_of(index)
        ]
        halves.append(jnp.concatenate(picked, axis=1))
    rows = jnp.concatenate(halves, axis=0)
    return jnp.where(inverse_row >= 0, rows, 0.0)


def start_coarse(blocks_ref, basis_ref, residual, rows_ref, send_ref):
    rows_ref[:TRACE, :] = residual
    totals = [None] * (FB // LANES)
    for a in range(TRACE):
        for t in range(len(totals)):
            lanes = slice(t * LANES, (t + 1) * LANES)
            term = basis_ref[a, :, lanes] * rows_ref[a : a + 1, lanes]
            totals[t] = term if totals[t] is None else totals[t] + term
    restricted = jnp.sum(totals[0] + totals[1] + totals[2], axis=1, keepdims=True)
    start = jnp.sum(blocks_ref[:CVEC, :] * as_row(restricted), axis=1, keepdims=True)
    send_ref[...] = jnp.broadcast_to(as_row(start, start), send_ref.shape)


def sweeps(couple_ref, link_ref, source, trace, live, interface, stack_ref, rows_ref, count):
    rows_ref[...] = trace
    trace = trace[:TRACE]
    for sweep in range(count + 1):
        residual = source - couple_apply(
            couple_ref, link_ref, rows_ref[...], live, interface, stack_ref
        )
        if sweep < count:
            trace = trace + omega_step * residual
            rows_ref[:TRACE, :] = trace
    return trace, residual


def place_rows(places):
    row = lax.broadcasted_iota(jnp.int32, (8, LANES), 0)
    low = lax.broadcasted_iota(jnp.int32, (8, LANES), 1) < CVEC
    out = jnp.zeros((8, LANES), jnp.int32)
    for k, (at_low, at_high) in enumerate(places):
        out = jnp.where(row == k, jnp.where(low, at_low, at_high), out)
    return out


def first_kernel(
    groups, peers,
    count_hbm, pairs_hbm, ids_hbm, slots_hbm, load_hbm, link_hbm, matrix_hbm, coupling_hbm, basis_hbm, couple_ref,
    trace_ref, load_out_ref, live_ref, inverse_ref, wide_ref, mine_ref, places_ref, blocks_ref, send_ref,
    stack_ref, rows_ref, count_ref, pairs_ref, ids_ref, slots_ref, load_ref, link_ref, matrix_ref, coupling_ref,
    basis_ref, sems,
):
    moves = [
        pltpu.make_async_copy(source, target, sems.at[at])
        for at, (source, target) in enumerate(
            [
                (count_hbm, count_ref),
                (pairs_hbm, pairs_ref),
                (ids_hbm, ids_ref),
                (slots_hbm, slots_ref),
                (load_hbm, load_ref),
                (link_hbm, link_ref),
                (matrix_hbm, matrix_ref),
                (coupling_hbm, coupling_ref),
                (basis_hbm, basis_ref),
            ]
        )
    ]
    for move in moves:
        move.start()
    group, own = lax.axis_index("grp"), lax.axis_index("sub")
    load_out_ref[...] = jnp.zeros_like(load_out_ref)
    for move in moves[:6]:
        move.wait()

    live = (lax.broadcasted_iota(jnp.int32, (1, FB), 1) < count_ref[0, 0]).astype(f32)
    live_ref[...] = live
    slots = slots_ref[...]
    wide_ref[...] = jnp.concatenate([slots] * (LANES // CAP), axis=1)
    lane = lax.broadcasted_iota(jnp.int32, (8, LANES), 1) // CAP
    mine_ref[...] = (lane == lax.rem(own, LANES // CAP)).astype(jnp.int32)
    columns = slots.T
    slot = lax.broadcasted_iota(jnp.int32, (CAP, FB), 0)
    face = lax.broadcasted_iota(jnp.int32, (CAP, FB), 1)
    found = jnp.zeros((CAP, FB), jnp.int32)
    for j in range(peers):
        named = (columns[:, j : j + 1] == face) & (slot < pairs_ref[0, j])
        found = found + jnp.where(named, slot + (j * CAP + 1), 0)
    inverse = jnp.sum(found, axis=0, keepdims=True) - 1
    inverse_ref[...] = inverse
    interface = (inverse >= 0).astype(f32)

    for a in range(TRACE):
        load_out_ref[a : a + 1, :] = load_ref[a]
    source = live * load_out_ref[...]
    start = omega_step * source
    trace, residual = sweeps(
        couple_ref, link_ref, source[:TRACE], start, live, interface, stack_ref, rows_ref, SWEEPS - 1
    )
    trace_ref[...] = start
    trace_ref[:TRACE, :] = trace

    rows = 2 * peers
    odd = lax.rem(group, 2)
    base = group - odd
    partner = lax.rem(jnp.where(odd == 1, group + 1, group + groups - 1), groups)
    partner_base = partner - lax.rem(partner, 2)

    def place(identity, pair, other):
        inside = (identity >= pair * peers) & (identity < pair * peers + rows)
        return jnp.clip(jnp.where(inside, identity - pair * peers, rows + identity - other * peers), 0, 2 * rows - 1)

    def second(k):
        identity = ids_ref[0, k]
        ahead = lax.div(identity, peers) - base
        across = ((ahead < 0) | (ahead > 1)).astype(jnp.int32)
        return jnp.where(ahead > 0, peers, 0) + lax.rem(identity, peers), across

    myself = group * peers + own
    for at, (pair, other) in enumerate(((base, partner_base), (partner_base, base))):
        spots = [place(ids_ref[0, k], pair, other) for k in range(KC)]
        spots = list(zip(spots[0::2], spots[1::2])) + [(place(myself, pair, other),) * 2]
        index = place_rows(spots)
        if at:
            blocks_ref[(KC // 2 + 1) * CVEC :, :] = index.astype(f32)
        else:
            places_ref[:8, :] = index
    spots = []
    for k in range(0, KC, 2):
        (row_low, across_low), (row_high, across_high) = second(k), second(k + 1)
        spots.append((row_low + rows * across_low, row_high + rows * (1 - across_high)))
    places_ref[8:, :] = place_rows(spots)

    for move in moves[6:]:
        move.wait()
    blocks_ref[:CVEC, :] = jnp.concatenate([matrix_ref[...], jnp.zeros((CVEC, CVEC), f32)], axis=1)
    for k in range(0, KC, 2):
        at = (k // 2 + 1) * CVEC
        blocks_ref[at : at + CVEC, :] = jnp.concatenate([coupling_ref[k], coupling_ref[k + 1]], axis=1)
    start_coarse(blocks_ref, basis_ref, residual, rows_ref, send_ref)


def local_kernel(
    arrived_ref, live_ref, inverse_ref, load_ref, link_ref, blocks_ref, old_ref, couple_ref, basis_ref,
    trace_ref, robin_ref, send_ref,
    stack_ref, rows_ref,
):
    live = live_ref[...]
    inverse = inverse_ref[...]
    interface = (inverse >= 0).astype(f32)
    robin = unpack_slots(arrived_ref, inverse)
    robin_ref[...] = robin
    source = live * (load_ref[...] + robin)
    trace, residual = sweeps(
        couple_ref, link_ref, source[:TRACE], old_ref[...], live, interface, stack_ref, rows_ref, SWEEPS
    )
    trace_ref[...] = robin
    trace_ref[:TRACE, :] = trace
    start_coarse(blocks_ref, basis_ref, residual, rows_ref, send_ref)


def coarse_step(blocks_ref, first, pair_rows):
    total = None
    for k in range(KC // 2):
        matrix = blocks_ref[first + (k + 1) * CVEC : first + (k + 2) * CVEC, :]
        term = matrix * pair_rows[k : k + 1]
        total = term if total is None else total + term
    coupled = jnp.sum(total, axis=1, keepdims=True)
    return jnp.sum(blocks_ref[first : first + CVEC, :] * as_row(coupled), axis=1, keepdims=True)


def sweep_kernel(places_ref, own_ref, partner_ref, blocks_ref, twin_ref, send_ref):
    rows = own_ref.shape[0]
    window = blocks_of(own_ref, rows) + blocks_of(partner_ref, rows)
    own = pick_rows(window, places_ref[:8, :])
    after = rows + (KC // 2 + 1) * CVEC
    twin = pick_rows(window, twin_ref[after : after + 8, :].astype(jnp.int32))
    steps = [coarse_step(blocks_ref, 0, own), coarse_step(twin_ref, rows, twin)]
    at = KC // 2
    swept = jnp.where(low_lanes(), own[at : at + 1], twin[at : at + 1]) - as_row(*steps)
    send_ref[...] = jnp.broadcast_to(swept, send_ref.shape)


def correct_kernel(
    first, last, places_ref, live_ref, mine_ref, start_ref, swept_ref, blocks_ref, slots_ref, trace_ref, *rest
):
    if first:
        basis_ref, *rest = rest
    else:
        robin_ref, basis_ref, *rest = rest
    if last:
        out_ref, coef_ref, packed_ref, rows_ref = rest
    else:
        out_ref, packed_ref, rows_ref = rest
    window = blocks_of(swept_ref, swept_ref.shape[0])
    window = window + [pltpu.roll(block, CVEC, 1) for block in window]
    step = coarse_step(blocks_ref, 0, pick_rows(window, places_ref[8:, :]))
    start = jnp.sum(jnp.where(eye(0), start_ref[:1, :], 0.0), axis=1, keepdims=True)
    column = start - step
    if last:
        coef_ref[...] = as_row(column)[:, :CVEC]
    spread = jnp.broadcast_to(column, (CVEC, LANES))
    live = live_ref[...]
    for a in range(TRACE):
        for t in range(FB // LANES):
            lanes = slice(t * LANES, (t + 1) * LANES)
            rows_ref[a : a + 1, lanes] = jnp.sum(basis_ref[a, :, lanes] * spread, axis=0, keepdims=True)
    rows_ref[TRACE:, :] = jnp.zeros((ROWS - TRACE, FB), f32)
    trace = trace_ref[...] + live * rows_ref[...]
    if last:
        for a in range(TRACE):
            out_ref[a] = trace[a : a + 1]
    else:
        out_ref[...] = trace
    outgoing = 2.0 * robin_weight * trace
    if not first:
        outgoing = outgoing - robin_ref[...]
    upper = tiles_of(outgoing[:8])
    lower = tiles_of(outgoing[8:])
    mine = mine_ref[...] > 0
    for j in range(slots_ref.shape[0]):
        index = jnp.broadcast_to(slots_ref[j : j + 1, :], (8, LANES))
        packed_ref[j * 8 : (j + 1) * 8, :] = jnp.where(mine, pick(upper, index), pick(lower, index))


def robin_kernel(arrived_ref, inverse_ref, out_ref):
    robin = unpack_slots(arrived_ref, inverse_ref[...])
    for a in range(TRACE):
        out_ref[a] = robin[a : a + 1]


VMEM = pl.BlockSpec(memory_space=pltpu.VMEM)


HBM = pl.BlockSpec(memory_space=pl.ANY)


def call(kernel, name, outs, scratch, operands, in_hbm=0):
    return pl.pallas_call(
        kernel,
        name=name,
        out_shape=[jax.ShapeDtypeStruct(shape, dtype) for shape, dtype in outs],
        in_specs=[HBM] * in_hbm + [VMEM] * (len(operands) - in_hbm),
        out_specs=[VMEM] * len(outs),
        scratch_shapes=scratch,
        compiler_params=pltpu.CompilerParams(vmem_limit_bytes=16 << 20),
    )(*operands)


def pair_groups(groups, peers):
    return [[(2 * m + h) * peers + s for h in range(2) for s in range(peers)] for m in range(groups // 2)]


def partner_pairs(groups):
    pairs = []
    for odd in range(1, groups - 1, 2):
        pairs += [(odd, odd + 1), (odd + 1, odd)]
    return pairs


def body(
    load, couple, face_link, face_count, slot_face, pair_count, basis, coarse_inverse, coarse_block, coarse_link
):
    groups, peers = lax.axis_size("grp"), lax.axis_size("sub")
    blocks = pair_groups(groups, peers)
    partners = partner_pairs(groups)
    rows = 2 * peers

    def exchange(send):
        arrived = lax.all_to_all(
            send.reshape(rows, 1, LANES), ("grp", "sub"), 0, 0, axis_index_groups=blocks, tiled=True
        )
        return arrived.reshape(rows, LANES)

    integer = jnp.int32
    field = ((ROWS, FB), f32)
    sends = ((rows, LANES), f32)
    output = ((TRACE, 1, FB), f32)
    packed_shape = ((KC // 2 + 1) * CVEC + 8, LANES)
    work = [pltpu.VMEM((LINKS + 1, ROWS, FB), f32), pltpu.VMEM((ROWS, FB), f32)]
    face_links = jnp.moveaxis(face_link[0], 0, 1)
    couple_rows = jnp.swapaxes(couple[0, 0], 1, 2)
    basis_rows = jnp.swapaxes(basis[0, 0], 0, 1)
    given = [
        (face_count, pltpu.SMEM),
        (pair_count[0], pltpu.SMEM),
        (coarse_link[0], pltpu.SMEM),
        (slot_face[0, 0], pltpu.VMEM),
        (jnp.moveaxis(load[0], 0, 1), pltpu.VMEM),
        (face_links, pltpu.VMEM),
        (coarse_inverse[0, 0], pltpu.VMEM),
        (coarse_block[0, 0], pltpu.VMEM),
        (basis_rows, pltpu.VMEM),
    ]
    trace, source, live, inverse, wide_slots, mine, places, packed, start = call(
        functools.partial(first_kernel, groups, peers),
        "first",
        [
            field,
            field,
            ((1, FB), f32),
            ((1, FB), integer),
            ((peers, LANES), integer),
            ((8, LANES), integer),
            ((16, LANES), integer),
            (packed_shape, f32),
            sends,
        ],
        work + [space(x.shape, x.dtype) for x, space in given] + [pltpu.SemaphoreType.DMA((len(given),))],
        [given[0][0]]
        + [pltpu.with_memory_space_constraint(x, pltpu.HBM) for x, space in given[1:]]
        + [couple_rows],
        len(given),
    )
    robin = arrived = twin = None
    for outer_step in range(ITERS):
        first, last = outer_step == 0, outer_step == ITERS - 1
        if not first:
            trace, robin, start = call(
                local_kernel,
                "local",
                [field, field, sends],
                work,
                [arrived, live, inverse, source, face_links, packed, trace, couple_rows, basis_rows],
            )
        window = exchange(start)
        if first:
            twin = beyond = lax.ppermute(jnp.concatenate([window, packed], axis=0), "grp", partners)
        else:
            beyond = lax.ppermute(window, "grp", partners)
        (swept,) = call(sweep_kernel, "sweep", [sends], [], [places, window, beyond, packed, twin])
        swept = exchange(swept)
        operands = [places, live, mine, start, swept, packed, wide_slots, trace]
        operands += ([] if first else [robin]) + [basis_rows]
        results = call(
            functools.partial(correct_kernel, first, last),
            "correct",
            ([output, ((1, CVEC), f32)] if last else [field]) + [((peers * 8, LANES), f32)],
            [pltpu.VMEM((ROWS, FB), f32)],
            operands,
        )
        trace, outgoing = results[0], results[-1]
        if last:
            coefficients = results[1]
        arrived = lax.all_to_all(outgoing.reshape(peers, 8, LANES), "sub", 0, 0, tiled=True)
        arrived = arrived.reshape(peers * 8, LANES)
    (robin,) = call(robin_kernel, "robin", [output], [], [arrived, inverse])
    return (jnp.moveaxis(trace, 0, 1)[None], jnp.moveaxis(robin, 0, 1)[None], coefficients[None])


def solution(mesh):
    in_specs = (
        P("grp", "sub", None, None),
        P("grp", "sub", None, None, None, None),
        P("grp", "sub", None, None),
        P("grp", "sub"),
        P("grp", "sub", None, None),
        P("grp", "sub", None),
        P("grp", "sub", None, None, None),
        P("grp", "sub", None, None),
        P("grp", "sub", None, None, None),
        P("grp", "sub", None),
    )
    out_specs = (P("grp", "sub", None, None), P("grp", "sub", None, None), P("grp", "sub", None))
    return jax.shard_map(body, mesh=mesh, in_specs=in_specs, out_specs=out_specs, check_vma=False)
```

```python
import functools

import jax
import jax.numpy as jnp
from jax import lax
from jax.experimental import pallas as pl
from jax.experimental.pallas import tpu as pltpu
from jax.sharding import PartitionSpec as P

TRACE = 15
ROWS = 16
FB = 384
CAP = 32
LANES = 128
LINKS = 3
CVEC = 64
KC = 6
ITERS = 3
SWEEPS = 2

robin_weight = 1.0
omega_step = 0.2
f32 = jnp.float32


def pick(pieces, index):
    low = jnp.bitwise_and(index, LANES - 1)
    high = jnp.right_shift(index, 7)
    out = None
    for at, piece in enumerate(pieces):
        taken = jnp.take_along_axis(piece, low, axis=1, mode="promise_in_bounds")
        out = taken if out is None else jnp.where(high == at, taken, out)
    return out


def tiles_of(rows):
    return [rows[:, t * LANES : (t + 1) * LANES] for t in range(rows.shape[1] // LANES)]


def pick_faces(rows, index_row):
    pieces = tiles_of(rows)
    picked = [
        pick(pieces, jnp.broadcast_to(part, (rows.shape[0], LANES))) for part in tiles_of(index_row)
    ]
    return jnp.concatenate(picked, axis=1)


def pick_rows(blocks, index):
    low = jnp.bitwise_and(index, 7)
    high = jnp.right_shift(index, 3)
    out = None
    for at, block in enumerate(blocks):
        taken = jnp.take_along_axis(block, low, axis=0, mode="promise_in_bounds")
        out = taken if out is None else jnp.where(high == at, taken, out)
    return out


def blocks_of(ref, rows):
    return [ref[at : at + 8, :] for at in range(0, rows, 8)]


def eye(offset):
    row = lax.broadcasted_iota(jnp.int32, (CVEC, LANES), 0)
    lane = lax.broadcasted_iota(jnp.int32, (CVEC, LANES), 1)
    return lane == row + offset


def as_row(low, high=None):
    spread = jnp.where(eye(0), low, 0.0)
    if high is not None:
        spread = spread + jnp.where(eye(CVEC), high, 0.0)
    return jnp.sum(spread, axis=0, keepdims=True)


def low_lanes():
    return lax.broadcasted_iota(jnp.int32, (1, LANES), 1) < CVEC


def couple_apply(couple_ref, link_ref, trace, live, interface, stack_ref):
    stack_ref[0] = trace
    for k in range(LINKS):
        stack_ref[k + 1] = pick_faces(trace, link_ref[k])
    sums = []
    for k in range(LINKS + 1):
        total = None
        for b in range(TRACE):
            term = couple_ref[k, b].astype(f32) * stack_ref[k, b : b + 1, :]
            total = term if total is None else total + term
        sums.append(total)
    total = (sums[0] + sums[1]) + (sums[2] + sums[3])
    return live * (total + robin_weight * interface * trace[:TRACE])


def unpack_slots(arrived_ref, inverse_row):
    lane = lax.broadcasted_iota(jnp.int32, (8, LANES), 1) // CAP
    per_tile = LANES // CAP
    count = arrived_ref.shape[0] // 8 // per_tile
    halves = []
    for half in range(2):
        pieces = []
        for tile in range(count):
            joined = None
            for m in range(per_tile):
                at = (tile * per_tile + m) * 8
                block = arrived_ref[at : at + 8, :]
                place = (m + 2 * half) % per_tile
                joined = block if joined is None else jnp.where(lane == place, block, joined)
            pieces.append(joined)
        index = jnp.maximum(inverse_row, 0)
        if half:
            index = jnp.bitwise_or(
                jnp.bitwise_and(index, -LANES), jnp.bitwise_and(index + LANES // 2, LANES - 1)
            )
        picked = [
            pick(pieces, jnp.broadcast_to(part, (8, LANES))) for part in tiles_of(index)
        ]
        halves.append(jnp.concatenate(picked, axis=1))
    rows = jnp.concatenate(halves, axis=0)
    return jnp.where(inverse_row >= 0, rows, 0.0)


def start_coarse(matrix_ref, basis_ref, residual, rows_ref, send_ref):
    rows_ref[:TRACE, :] = residual
    totals = [None] * (FB // LANES)
    for a in range(TRACE):
        for t in range(len(totals)):
            lanes = slice(t * LANES, (t + 1) * LANES)
            term = basis_ref[a, :, lanes] * rows_ref[a : a + 1, lanes]
            totals[t] = term if totals[t] is None else totals[t] + term
    restricted = jnp.sum(totals[0] + totals[1] + totals[2], axis=1, keepdims=True)
    start = jnp.sum(matrix_ref[...] * as_row(restricted)[:, :CVEC], axis=1, keepdims=True)
    send_ref[...] = jnp.broadcast_to(as_row(start, start), send_ref.shape)


def sweeps(couple_ref, link_ref, source, trace, live, interface, stack_ref, rows_ref, count):
    rows_ref[...] = trace
    trace = trace[:TRACE]
    for sweep in range(count + 1):
        residual = source - couple_apply(
            couple_ref, link_ref, rows_ref[...], live, interface, stack_ref
        )
        if sweep < count:
            trace = trace + omega_step * residual
            rows_ref[:TRACE, :] = trace
    return trace, residual


def place_rows(places):
    row = lax.broadcasted_iota(jnp.int32, (8, LANES), 0)
    low = lax.broadcasted_iota(jnp.int32, (8, LANES), 1) < CVEC
    out = jnp.zeros((8, LANES), jnp.int32)
    for k, (at_low, at_high) in enumerate(places):
        out = jnp.where(row == k, jnp.where(low, at_low, at_high), out)
    return out


def first_kernel(
    groups, peers,
    count_hbm, pairs_hbm, ids_hbm, slots_hbm, load_hbm, link_hbm, matrix_hbm, coupling_hbm, basis_hbm, couple_ref,
    trace_ref, load_out_ref, live_ref, inverse_ref, wide_ref, mine_ref, places_ref, blocks_ref, send_ref,
    stack_ref, rows_ref, count_ref, pairs_ref, ids_ref, slots_ref, load_ref, link_ref, matrix_ref, coupling_ref,
    basis_ref, sems,
):
    moves = [
        pltpu.make_async_copy(source, target, sems.at[at])
        for at, (source, target) in enumerate(
            [
                (count_hbm, count_ref),
                (pairs_hbm, pairs_ref),
                (ids_hbm, ids_ref),
                (slots_hbm, slots_ref),
                (load_hbm, load_ref),
                (link_hbm, link_ref),
                (matrix_hbm, matrix_ref),
                (coupling_hbm, coupling_ref),
                (basis_hbm, basis_ref),
            ]
        )
    ]
    for move in moves:
        move.start()
    group, own = lax.axis_index("grp"), lax.axis_index("sub")
    load_out_ref[...] = jnp.zeros_like(load_out_ref)
    for move in moves[:6]:
        move.wait()

    live = (lax.broadcasted_iota(jnp.int32, (1, FB), 1) < count_ref[0, 0]).astype(f32)
    live_ref[...] = live
    slots = slots_ref[...]
    wide_ref[...] = jnp.concatenate([slots] * (LANES // CAP), axis=1)
    lane = lax.broadcasted_iota(jnp.int32, (8, LANES), 1) // CAP
    mine_ref[...] = (lane == lax.rem(own, LANES // CAP)).astype(jnp.int32)
    columns = slots.T
    slot = lax.broadcasted_iota(jnp.int32, (CAP, FB), 0)
    face = lax.broadcasted_iota(jnp.int32, (CAP, FB), 1)
    found = jnp.zeros((CAP, FB), jnp.int32)
    for j in range(peers):
        named = (columns[:, j : j + 1] == face) & (slot < pairs_ref[0, j])
        found = found + jnp.where(named, slot + (j * CAP + 1), 0)
    inverse = jnp.sum(found, axis=0, keepdims=True) - 1
    inverse_ref[...] = inverse
    interface = (inverse >= 0).astype(f32)

    for a in range(TRACE):
        load_out_ref[a : a + 1, :] = load_ref[a]
    source = live * load_out_ref[...]
    start = omega_step * source
    trace, residual = sweeps(
        couple_ref, link_ref, source[:TRACE], start, live, interface, stack_ref, rows_ref, SWEEPS - 1
    )
    trace_ref[...] = start
    trace_ref[:TRACE, :] = trace

    rows = 2 * peers
    odd = lax.rem(group, 2)
    base = group - odd
    partner = lax.rem(jnp.where(odd == 1, group + 1, group + groups - 1), groups)
    partner_base = partner - lax.rem(partner, 2)

    def place(identity, pair, other):
        inside = (identity >= pair * peers) & (identity < pair * peers + rows)
        return jnp.clip(jnp.where(inside, identity - pair * peers, rows + identity - other * peers), 0, 2 * rows - 1)

    def second(k):
        identity = ids_ref[0, k]
        ahead = lax.div(identity, peers) - base
        across = ((ahead < 0) | (ahead > 1)).astype(jnp.int32)
        return jnp.where(ahead > 0, peers, 0) + lax.rem(identity, peers), across

    myself = group * peers + own
    for at, (pair, other) in enumerate(((base, partner_base), (partner_base, base))):
        spots = [place(ids_ref[0, k], pair, other) for k in range(KC)]
        spots = list(zip(spots[0::2], spots[1::2])) + [(place(myself, pair, other),) * 2]
        index = place_rows(spots)
        if at:
            blocks_ref[KC // 2 * CVEC :, :] = index.astype(f32)
        else:
            places_ref[:8, :] = index
    spots = []
    for k in range(0, KC, 2):
        (row_low, across_low), (row_high, across_high) = second(k), second(k + 1)
        spots.append((row_low + rows * across_low, row_high + rows * (1 - across_high)))
    places_ref[8:, :] = place_rows(spots)

    for move in moves[6:]:
        move.wait()
    matrix = matrix_ref[...]
    for k in range(0, KC, 2):
        at = k // 2 * CVEC
        pair = jnp.concatenate([coupling_ref[k], coupling_ref[k + 1]], axis=1)
        blocks_ref[at : at + CVEC, :] = jnp.dot(
            matrix, pair, precision=lax.Precision.HIGHEST, preferred_element_type=f32
        )
    start_coarse(matrix_ref, basis_ref, residual, rows_ref, send_ref)


def local_kernel(
    arrived_ref, live_ref, inverse_ref, load_ref, link_ref, matrix_ref, old_ref, couple_ref, basis_ref,
    trace_ref, robin_ref, send_ref,
    stack_ref, rows_ref,
):
    live = live_ref[...]
    inverse = inverse_ref[...]
    interface = (inverse >= 0).astype(f32)
    robin = unpack_slots(arrived_ref, inverse)
    robin_ref[...] = robin
    source = live * (load_ref[...] + robin)
    trace, residual = sweeps(
        couple_ref, link_ref, source[:TRACE], old_ref[...], live, interface, stack_ref, rows_ref, SWEEPS
    )
    trace_ref[...] = robin
    trace_ref[:TRACE, :] = trace
    start_coarse(matrix_ref, basis_ref, residual, rows_ref, send_ref)


def coarse_step(blocks_ref, first, pair_rows):
    total = None
    for k in range(KC // 2):
        matrix = blocks_ref[first + k * CVEC : first + (k + 1) * CVEC, :]
        term = matrix * pair_rows[k : k + 1]
        total = term if total is None else total + term
    return jnp.sum(total, axis=1, keepdims=True)


def sweep_kernel(places_ref, own_ref, partner_ref, blocks_ref, twin_ref, send_ref):
    rows = own_ref.shape[0]
    window = blocks_of(own_ref, rows) + blocks_of(partner_ref, rows)
    own = pick_rows(window, places_ref[:8, :])
    after = rows + KC // 2 * CVEC
    twin = pick_rows(window, twin_ref[after : after + 8, :].astype(jnp.int32))
    steps = [coarse_step(blocks_ref, 0, own), coarse_step(twin_ref, rows, twin)]
    at = KC // 2
    swept = jnp.where(low_lanes(), own[at : at + 1], twin[at : at + 1]) - as_row(*steps)
    send_ref[...] = jnp.broadcast_to(swept, send_ref.shape)


def correct_kernel(
    first, last, places_ref, live_ref, mine_ref, start_ref, swept_ref, blocks_ref, slots_ref, trace_ref, *rest
):
    if first:
        basis_ref, *rest = rest
    else:
        robin_ref, basis_ref, *rest = rest
    if last:
        out_ref, coef_ref, packed_ref, rows_ref = rest
    else:
        out_ref, packed_ref, rows_ref = rest
    window = blocks_of(swept_ref, swept_ref.shape[0])
    window = window + [pltpu.roll(block, CVEC, 1) for block in window]
    step = coarse_step(blocks_ref, 0, pick_rows(window, places_ref[8:, :]))
    start = jnp.sum(jnp.where(eye(0), start_ref[:1, :], 0.0), axis=1, keepdims=True)
    column = start - step
    if last:
        coef_ref[...] = as_row(column)[:, :CVEC]
    spread = jnp.broadcast_to(column, (CVEC, LANES))
    live = live_ref[...]
    for a in range(TRACE):
        for t in range(FB // LANES):
            lanes = slice(t * LANES, (t + 1) * LANES)
            rows_ref[a : a + 1, lanes] = jnp.sum(basis_ref[a, :, lanes] * spread, axis=0, keepdims=True)
    rows_ref[TRACE:, :] = jnp.zeros((ROWS - TRACE, FB), f32)
    trace = trace_ref[...] + live * rows_ref[...]
    out_ref[...] = trace
    outgoing = 2.0 * robin_weight * trace
    if not first:
        outgoing = outgoing - robin_ref[...]
    upper = tiles_of(outgoing[:8])
    lower = tiles_of(outgoing[8:])
    mine = mine_ref[...] > 0
    for j in range(slots_ref.shape[0]):
        index = jnp.broadcast_to(slots_ref[j : j + 1, :], (8, LANES))
        packed_ref[j * 8 : (j + 1) * 8, :] = jnp.where(mine, pick(upper, index), pick(lower, index))


def robin_kernel(
    trace_ref, arrived_ref, inverse_ref, trace_hbm, robin_hbm, trace_rows, robin_rows, sems
):
    moves = []

    def put(values, rows_ref, target):
        for a in range(TRACE):
            rows_ref[a] = values[a : a + 1]
        moves.append(pltpu.make_async_copy(rows_ref, target, sems.at[len(moves)]))
        moves[-1].start()

    put(trace_ref[...], trace_rows, trace_hbm)
    put(unpack_slots(arrived_ref, inverse_ref[...]), robin_rows, robin_hbm)
    for move in moves:
        move.wait()


VMEM = pl.BlockSpec(memory_space=pltpu.VMEM)


HBM = pl.BlockSpec(memory_space=pl.ANY)


def call(kernel, name, outs, scratch, operands, in_hbm=0, out_hbm=0):
    return pl.pallas_call(
        kernel,
        name=name,
        out_shape=[jax.ShapeDtypeStruct(shape, dtype) for shape, dtype in outs],
        in_specs=[HBM] * in_hbm + [VMEM] * (len(operands) - in_hbm),
        out_specs=[HBM] * out_hbm + [VMEM] * (len(outs) - out_hbm),
        scratch_shapes=scratch,
        compiler_params=pltpu.CompilerParams(vmem_limit_bytes=16 << 20),
    )(*operands)


def pair_groups(groups, peers):
    return [[(2 * m + h) * peers + s for h in range(2) for s in range(peers)] for m in range(groups // 2)]


def partner_pairs(groups):
    pairs = []
    for odd in range(1, groups - 1, 2):
        pairs += [(odd, odd + 1), (odd + 1, odd)]
    return pairs


def body(
    load, couple, face_link, face_count, slot_face, pair_count, basis, coarse_inverse, coarse_block, coarse_link
):
    groups, peers = lax.axis_size("grp"), lax.axis_size("sub")
    blocks = pair_groups(groups, peers)
    partners = partner_pairs(groups)
    rows = 2 * peers

    def exchange(send):
        arrived = lax.all_to_all(
            send.reshape(rows, 1, LANES), ("grp", "sub"), 0, 0, axis_index_groups=blocks, tiled=True
        )
        return arrived.reshape(rows, LANES)

    integer = jnp.int32
    field = ((ROWS, FB), f32)
    sends = ((rows, LANES), f32)
    output = ((TRACE, 1, FB), f32)
    packed_shape = (KC // 2 * CVEC + 8, LANES)
    work = [pltpu.VMEM((LINKS + 1, ROWS, FB), f32), pltpu.VMEM((ROWS, FB), f32)]
    face_links = jnp.moveaxis(face_link[0], 0, 1)
    couple_rows = jnp.swapaxes(couple[0, 0], 1, 2).astype(f32)
    basis_rows = jnp.swapaxes(basis[0, 0], 0, 1)
    given = [
        (face_count, pltpu.SMEM),
        (pair_count[0], pltpu.SMEM),
        (coarse_link[0], pltpu.SMEM),
        (slot_face[0, 0], pltpu.VMEM),
        (jnp.moveaxis(load[0], 0, 1), pltpu.VMEM),
        (face_links, pltpu.VMEM),
        (coarse_inverse[0, 0], pltpu.VMEM),
        (coarse_block[0, 0], pltpu.VMEM),
        (basis_rows, pltpu.VMEM),
    ]
    trace, source, live, inverse, wide_slots, mine, places, packed, start = call(
        functools.partial(first_kernel, groups, peers),
        "first",
        [
            field,
            field,
            ((1, FB), f32),
            ((1, FB), integer),
            ((peers, LANES), integer),
            ((8, LANES), integer),
            ((16, LANES), integer),
            (packed_shape, f32),
            sends,
        ],
        work + [space(x.shape, x.dtype) for x, space in given] + [pltpu.SemaphoreType.DMA((len(given),))],
        [given[0][0]]
        + [pltpu.with_memory_space_constraint(x, pltpu.HBM) for x, space in given[1:]]
        + [couple_rows],
        len(given),
    )
    robin = arrived = twin = None
    for outer_step in range(ITERS):
        first, last = outer_step == 0, outer_step == ITERS - 1
        if not first:
            trace, robin, start = call(
                local_kernel,
                "local",
                [field, field, sends],
                work,
                [
                    arrived, live, inverse, source, face_links, coarse_inverse[0, 0], trace, couple_rows, basis_rows
                ],
            )
        window = exchange(start)
        if first:
            twin = beyond = lax.ppermute(jnp.concatenate([window, packed], axis=0), "grp", partners)
        else:
            beyond = lax.ppermute(window, "grp", partners)
        (swept,) = call(sweep_kernel, "sweep", [sends], [], [places, window, beyond, packed, twin])
        swept = exchange(swept)
        operands = [places, live, mine, start, swept, packed, wide_slots, trace]
        operands += ([] if first else [robin]) + [basis_rows]
        results = call(
            functools.partial(correct_kernel, first, last),
            "correct",
            [field] + ([((1, CVEC), f32)] if last else []) + [((peers * 8, LANES), f32)],
            [pltpu.VMEM((ROWS, FB), f32)],
            operands,
        )
        trace, outgoing = results[0], results[-1]
        if last:
            coefficients = results[1]
        arrived = lax.all_to_all(outgoing.reshape(peers, 8, LANES), "sub", 0, 0, tiled=True)
        arrived = arrived.reshape(peers * 8, LANES)
    trace, robin = call(
        robin_kernel,
        "robin",
        [output, output],
        [pltpu.VMEM(*output), pltpu.VMEM(*output), pltpu.SemaphoreType.DMA((2,))],
        [trace, arrived, inverse],
        out_hbm=2,
    )
    return (jnp.moveaxis(trace, 0, 1)[None], jnp.moveaxis(robin, 0, 1)[None], coefficients[None])


def solution(mesh):
    in_specs = (
        P("grp", "sub", None, None),
        P("grp", "sub", None, None, None, None),
        P("grp", "sub", None, None),
        P("grp", "sub"),
        P("grp", "sub", None, None),
        P("grp", "sub", None),
        P("grp", "sub", None, None, None),
        P("grp", "sub", None, None),
        P("grp", "sub", None, None, None),
        P("grp", "sub", None),
    )
    out_specs = (P("grp", "sub", None, None), P("grp", "sub", None, None), P("grp", "sub", None))
    return jax.shard_map(body, mesh=mesh, in_specs=in_specs, out_specs=out_specs, check_vma=False)
```
